32 devices in a mesh: ctx: 16 (over z, y, core), tp: 2 (over x).
Axes of the slice: x: 2, y: 2, z: 4, core: 2. Of those that a mesh axis runs over, the one named last changes fastest.
Arguments:
- attn_q: bfloat16 [4096, 2048], P('ctx', 'tp'), may hold values from -5 to 5
- attn_k: bfloat16 [4096, 2048], P('ctx', 'tp'), may hold values from -5 to 5
- attn_v: bfloat16 [4096, 2048], P('ctx', 'tp'), may hold values from -6 to 6
- attn_o: bfloat16 [4096, 2048], P('ctx', 'tp'), may hold values from -6 to 6
- attn_dy: bfloat16 [4096, 8192], P('ctx', 'tp'), may hold values from -6 to 6
- out_weight: bfloat16 [2048, 8192], P('tp'), may hold values from -0.0625 to 0.0625
- block_place: int32 [32], replicated, may hold values from 0 to 31, each once
- hyena_q: bfloat16 [4096, 4096], P('ctx', 'tp'), may hold values from -6 to 6
- hyena_k: bfloat16 [4096, 4096], P('ctx', 'tp'), may hold values from -6 to 6
- hyena_v: bfloat16 [4096, 4096], P('ctx', 'tp'), may hold values from -6 to 6
- hyena_dy: bfloat16 [4096, 4096], P('ctx', 'tp'), may hold values from -6 to 6
- filter_residue: float32 [16, 32], P(None, 'tp')
- filter_rate: float32 [16, 32], P(None, 'tp'), as said below
Outputs:
- grad_q_attn: bfloat16 [4096, 2048], P('ctx', 'tp')
- grad_k_attn: bfloat16 [4096, 2048], P('ctx', 'tp')
- grad_v_attn: bfloat16 [4096, 2048], P('ctx', 'tp')
- grad_q_hyena: bfloat16 [4096, 4096], P('ctx', 'tp')
- grad_k_hyena: bfloat16 [4096, 4096], P('ctx', 'tp')
- grad_v_hyena: bfloat16 [4096, 4096], P('ctx', 'tp')
The draws below stay inside these ranges and needn't reach their ends.
Inputs may be any that keep to these rules, and one draw needn't show every extreme that they name: A permutation of the 32 block places; index d of ctx holds, as its 256 rows of every attention array, the blocks at places block_place[2 d] and block_place[2 d + 1], in that order. `filter_rate`: positive, at most 1/30.
All inputs are finite; a program needn't handle non-finite values.
Results may differ from the reference program's by a relative error of at most 0.009.
Values may be sent and summed in bfloat16 or wider, within the bound.
A program may use at most 256 MiB of HBM per device.

```python
import math
import jax
import jax.numpy as jnp
from jax import lax

D = 8192
HD = 128
HEADS = 16
CHAN = 4096
GS = 128
MODES = 16
TOK_DEV = 256
TOKENS = 4096
BLOCKS = 32
N_CTX = 16


def filter_parts(key):
    grid_dims = (MODES, CHAN // GS)
    slow_pick = jax.random.randint(jax.random.fold_in(key, 11), grid_dims, 0, 2) == 1
    mixing = jax.random.uniform(jax.random.fold_in(key, 12), grid_dims, jnp.float32)
    slow_rate = 0.3 / TOKENS * jnp.exp(mixing * math.log(20.0 / 3.0))
    fast_rate = 1.0 / 50.0 * jnp.exp(mixing * math.log(50.0 / 30.0))
    rate_all = jnp.where(slow_pick, slow_rate, fast_rate)
    residue_all = jax.random.normal(jax.random.fold_in(key, 13), grid_dims, jnp.float32) * jnp.sqrt(2.0 * rate_all) * 0.5
    return (rate_all, residue_all)


def draw_filter_rate(key, part):
    return filter_parts(key)[0].astype(jnp.float32)


def draw_filter_residue(key, part):
    return filter_parts(key)[1].astype(jnp.float32)


def base_values(key, salt):
    feat_all = HEADS * HD
    return jnp.clip(jax.random.normal(jax.random.fold_in(key, salt), (TOKENS, feat_all), jnp.float32), -4.5, 4.5)


def draw_attn_q(key, part):
    values_base = base_values(key, 1)
    return values_base.astype(jnp.bfloat16)


def draw_attn_k(key, part):
    values_base = base_values(key, 2)
    return values_base.astype(jnp.bfloat16)


def shard_levels(rng, shape, split, low, largest):
    def one(dim, parts):
        draws = jax.random.uniform(jax.random.fold_in(jax.random.fold_in(rng, 6), dim), (parts,), jnp.float32, low / len(split), largest / len(split))
        return jnp.repeat(jnp.exp(draws), shape[dim] // parts).reshape((-1,) + (1,) * (len(shape) - dim - 1))

    level = one(*split[0])
    for cut in split[1:]:
        level = level * one(*cut)
    return level


def scatter_about(rng, extent, spread, bound, shards=(), kind=jnp.bfloat16):
    result = spread * jax.random.normal(rng, extent, jnp.float32)
    if shards:
        result = result * shard_levels(rng, extent, shards, -0.22, 0.18)
    return jnp.clip(result, -bound, bound).astype(kind)


def setup_inputs(seed: int = 0) -> dict:
    arg_keys = jax.random.split(jax.random.key(seed), 14)
    attn_q = draw_attn_q(jax.random.fold_in(arg_keys[13], 71), 0)
    attn_k = draw_attn_k(jax.random.fold_in(arg_keys[13], 71), 0)
    attn_v = scatter_about(arg_keys[2], (TOKENS, HEADS * HD), 1.0, 6.0, ((0, 16), (1, 2)))
    attn_o = scatter_about(arg_keys[3], (TOKENS, HEADS * HD), 1.0, 6.0, ((0, 16), (1, 2)))
    attn_dy = scatter_about(arg_keys[4], (TOKENS, D), 1.0, 6.0, ((0, 16), (1, 2)))
    out_weight = scatter_about(arg_keys[5], (HEADS * HD, D), D ** -0.5, 0.0625, ((0, 2),))
    block_place = jax.random.permutation(arg_keys[6], BLOCKS).astype(jnp.int32)
    hyena_q = scatter_about(arg_keys[7], (TOKENS, CHAN), 1.0, 6.0, ((0, 16), (1, 2)))
    hyena_k = scatter_about(arg_keys[8], (TOKENS, CHAN), 1.0, 6.0, ((0, 16), (1, 2)))
    hyena_v = scatter_about(arg_keys[9], (TOKENS, CHAN), 1.0, 6.0, ((0, 16), (1, 2)))
    hyena_dy = scatter_about(arg_keys[10], (TOKENS, CHAN), 1.0, 6.0, ((0, 16), (1, 2)))
    filter_residue = draw_filter_residue(jax.random.fold_in(arg_keys[13], 71), 0)
    filter_rate = draw_filter_rate(jax.random.fold_in(arg_keys[13], 71), 0)
    return dict(attn_q=attn_q, attn_k=attn_k, attn_v=attn_v, attn_o=attn_o, attn_dy=attn_dy, out_weight=out_weight, block_place=block_place, hyena_q=hyena_q, hyena_k=hyena_k, hyena_v=hyena_v, hyena_dy=hyena_dy, filter_residue=filter_residue, filter_rate=filter_rate)


def toeplitz_rows(filter_taps):
    groups, block_len = filter_taps.shape
    padded = jnp.concatenate([jnp.zeros_like(filter_taps), filter_taps], axis=1)[:, ::-1]
    flattened = jnp.tile(padded, (1, block_len))[:, :block_len * (2 * block_len - 1)]
    return flattened.reshape(groups, block_len, 2 * block_len - 1)[:, :, block_len - 1:]


def hyena_tables(filter_residue, filter_rate, block_len):
    lag_ids = jnp.arange(block_len).astype(jnp.float32)
    rate_col = filter_rate[:, :, None]
    head_decay = jnp.exp(-rate_col * lag_ids)
    filter_taps = jnp.einsum('mg,mgl->gl', filter_residue, head_decay, precision=lax.Precision.HIGHEST)
    tail_decay = jnp.exp(-rate_col * (block_len - 1 - lag_ids))
    into_block = filter_residue[:, :, None] * jnp.exp(-rate_col * (lag_ids + 1.0))
    back_block = filter_residue[:, :, None] * jnp.exp(-rate_col * (block_len - lag_ids))
    block_decay = jnp.exp(-filter_rate * block_len)
    return toeplitz_rows(filter_taps), tail_decay, head_decay, into_block, back_block, block_decay


def hyena_grads(hyena_q, hyena_k, hyena_v, hyena_dy, filter_residue, filter_rate):
    groups = CHAN // GS
    block_shape = (N_CTX, TOK_DEV, groups, GS)
    prod_kv = (hyena_k.astype(jnp.float32) * hyena_v.astype(jnp.float32)).reshape(block_shape)
    prod_qdy = (hyena_q.astype(jnp.float32) * hyena_dy.astype(jnp.float32)).reshape(block_shape)
    toeplitz, tail_decay, head_decay, into_block, back_block, block_decay = hyena_tables(filter_residue, filter_rate, TOK_DEV)
    decay_col = block_decay[:, :, None]
    highest = lax.Precision.HIGHEST

    def forward_step(state, prod_blk):
        conv = jnp.einsum('gts,sgc->tgc', toeplitz, prod_blk, precision=highest)
        conv = conv + jnp.einsum('mgt,mgc->tgc', into_block, state, precision=highest)
        state = decay_col * state + jnp.einsum('mgs,sgc->mgc', tail_decay, prod_blk, precision=highest)
        return state, conv

    def backward_step(state, prod_blk):
        grad_mid = jnp.einsum('gts,tgc->sgc', toeplitz, prod_blk, precision=highest)
        grad_mid = grad_mid + jnp.einsum('mgs,mgc->sgc', back_block, state, precision=highest)
        state = decay_col * state + jnp.einsum('mgt,tgc->mgc', head_decay, prod_blk, precision=highest)
        return state, grad_mid

    zero_state = jnp.zeros((MODES, groups, GS), jnp.float32)
    _, conv = lax.scan(forward_step, zero_state, prod_kv)
    _, grad_mid = lax.scan(backward_step, zero_state, prod_qdy, reverse=True)
    conv = conv.reshape(TOKENS, CHAN)
    grad_mid = grad_mid.reshape(TOKENS, CHAN)
    grad_q = (hyena_dy.astype(jnp.float32) * conv).astype(jnp.bfloat16)
    grad_k = (grad_mid * hyena_v.astype(jnp.float32)).astype(jnp.bfloat16)
    grad_v = (grad_mid * hyena_k.astype(jnp.float32)).astype(jnp.bfloat16)
    return grad_q, grad_k, grad_v


def attention_grads(attn_q, attn_k, attn_v, attn_o, attn_dy, out_weight, block_place):
    block_len = TOK_DEV // 2
    row_ids = jnp.arange(TOKENS).astype(jnp.int32)
    seq_place = (block_place[row_ids // block_len] * block_len + row_ids % block_len).astype(jnp.int32)
    order_rows = jnp.zeros((TOKENS,), jnp.int32).at[seq_place].set(row_ids)
    grad_out = jnp.dot(attn_dy, out_weight.T, preferred_element_type=jnp.float32).astype(jnp.bfloat16)
    delta = jnp.sum((grad_out.astype(jnp.float32) * attn_o.astype(jnp.float32)).reshape(TOKENS, HEADS, HD), axis=2)

    def ordered(array):
        return array[order_rows].reshape(TOKENS, HEADS, HD).astype(jnp.float32)

    q_seq = ordered(attn_q)
    k_seq = ordered(attn_k)
    v_seq = ordered(attn_v)
    grad_seq = ordered(grad_out)
    delta_seq = delta[order_rows]
    softmax_scale = HD ** -0.5
    block_rows = 4 * TOK_DEV
    grad_q_parts = []
    grad_k_seq = jnp.zeros((TOKENS, HEADS, HD), jnp.float32)
    grad_v_seq = jnp.zeros((TOKENS, HEADS, HD), jnp.float32)
    for block_id in range(TOKENS // block_rows):
        row_start = block_id * block_rows
        row_end = row_start + block_rows
        query_blk = q_seq[row_start:row_end]
        grad_blk = grad_seq[row_start:row_end]
        key_blk = k_seq[:row_end]
        value_blk = v_seq[:row_end]
        scores = jnp.einsum('qhd,khd->hqk', query_blk, key_blk) * softmax_scale
        visible = jnp.arange(row_end)[None, :] <= jnp.arange(row_start, row_end)[:, None]
        scores = jnp.where(visible[None], scores, -jnp.inf)
        row_peak = jnp.max(scores, axis=2, keepdims=True)
        log_total = row_peak + jnp.log(jnp.sum(jnp.exp(scores - row_peak), axis=2, keepdims=True))
        probs_full = jnp.exp(scores - log_total)
        probs_low = lax.optimization_barrier(probs_full.astype(jnp.bfloat16)).astype(jnp.float32)
        grad_prob = jnp.einsum('qhd,khd->hqk', grad_blk, value_blk)
        delta_blk = delta_seq[row_start:row_end].T[:, :, None]
        grad_score = probs_full * (grad_prob - delta_blk)
        grad_score = lax.optimization_barrier(grad_score.astype(jnp.bfloat16)).astype(jnp.float32)
        grad_q_parts.append(jnp.einsum('hqk,khd->qhd', grad_score, key_blk) * softmax_scale)
        grad_k_seq = grad_k_seq.at[:row_end].add(jnp.einsum('hqk,qhd->khd', grad_score, query_blk) * softmax_scale)
        grad_v_seq = grad_v_seq.at[:row_end].add(jnp.einsum('hqk,qhd->khd', probs_low, grad_blk))
    grad_q_seq = jnp.concatenate(grad_q_parts, axis=0)

    def stored(array):
        return array[seq_place].reshape(TOKENS, HEADS * HD).astype(jnp.bfloat16)

    return stored(grad_q_seq), stored(grad_k_seq), stored(grad_v_seq)


def reference(attn_q, attn_k, attn_v, attn_o, attn_dy, out_weight, block_place, hyena_q, hyena_k, hyena_v, hyena_dy, filter_residue, filter_rate):
    attention = attention_grads(attn_q, attn_k, attn_v, attn_o, attn_dy, out_weight, block_place)
    hyena = hyena_grads(hyena_q, hyena_k, hyena_v, hyena_dy, filter_residue, filter_rate)
    return (attention[0], attention[1], attention[2], hyena[0], hyena[1], hyena[2])
```

```python
import functools
import math

import jax
import jax.numpy as jnp
from jax import lax
from jax.experimental import pallas as pl
from jax.experimental.pallas import tpu as pltpu
from jax.sharding import PartitionSpec as P

HD = 128
NEG_LARGE = -1e30
F32 = jnp.float32
BF16 = jnp.bfloat16
VMEM = pltpu.MemorySpace.VMEM
SMEM = pltpu.MemorySpace.SMEM


def dot_nn(a, b, precision=None):
    return lax.dot_general(
        a, b, (((1,), (0,)), ((), ())), precision=precision, preferred_element_type=F32
    )


def dot_nt(a, b):
    return lax.dot_general(a, b, (((1,), (1,)), ((), ())), preferred_element_type=F32)


def wide(x, length):
    return jnp.concatenate([x] * (length // x.shape[1]), axis=1)


def state_kernel(rate_ref, q_ref, k_ref, v_ref, dy_ref, out_ref):
    length = q_ref.shape[0]
    highest = lax.Precision.HIGHEST
    rate = wide(rate_ref[0], length)
    lag = lax.broadcasted_iota(jnp.int32, rate.shape, 1).astype(F32)
    prod_kv = k_ref[...].astype(F32) * v_ref[...].astype(F32)
    prod_qdy = q_ref[...].astype(F32) * dy_ref[...].astype(F32)
    tail = jnp.exp(-rate * (length - 1 - lag))
    head = jnp.exp(-rate * lag)
    out_ref[0, 0] = dot_nn(tail, prod_kv, highest)
    out_ref[0, 1] = dot_nn(head, prod_qdy, highest)


def mix_kernel(
    me_ref, rate_ref, res_ref, all_ref, q_ref, k_ref, v_ref, dy_ref, gq_ref, gk_ref, gv_ref
):
    length = q_ref.shape[0]
    count = all_ref.shape[0]
    highest = lax.Precision.HIGHEST
    me = me_ref[0]
    rate_b = rate_ref[0]
    state_in = jnp.zeros(rate_b.shape, F32)
    state_back = jnp.zeros(rate_b.shape, F32)
    for at in range(count):
        gap = me - 1 - at
        weight = jnp.exp(-rate_b * (length * jnp.maximum(gap, 0)).astype(F32))
        state_in = state_in + jnp.where(gap >= 0, weight, 0.0) * all_ref[at, 0, 0]
        gap = at - 1 - me
        weight = jnp.exp(-rate_b * (length * jnp.maximum(gap, 0)).astype(F32))
        state_back = state_back + jnp.where(gap >= 0, weight, 0.0) * all_ref[at, 0, 1]
    rate = wide(rate_b, length)
    res = wide(res_ref[0], length)
    lag_id = lax.broadcasted_iota(jnp.int32, rate.shape, 1)
    lag = lag_id.astype(F32)
    turned = jnp.where(lag_id == 0, 0, length - lag_id).astype(F32)
    taps = jnp.sum(res * jnp.exp(-rate * lag), axis=0, keepdims=True)
    taps_turned = jnp.sum(res * jnp.exp(-rate * turned), axis=0, keepdims=True)
    square = (length, length)
    row = lax.broadcasted_iota(jnp.int32, square, 0)
    col = lax.broadcasted_iota(jnp.int32, square, 1)
    lower = pltpu.roll(jnp.broadcast_to(taps_turned, square), 0, 1, stride=1, stride_axis=0)
    lower = jnp.where(col <= row, lower, 0.0)
    upper = pltpu.roll(jnp.broadcast_to(taps, square), 0, 1, stride=1, stride_axis=0)
    upper = jnp.where(col >= row, upper, 0.0)
    into = (res * jnp.exp(-rate * (lag + 1.0))).T
    back = (res * jnp.exp(-rate * (length - lag))).T
    k = k_ref[...].astype(F32)
    v = v_ref[...].astype(F32)
    dy = dy_ref[...].astype(F32)
    conv = dot_nn(lower, k * v, highest) + dot_nn(into, state_in, highest)
    mid = dot_nn(upper, q_ref[...].astype(F32) * dy, highest) + dot_nn(back, state_back, highest)
    gq_ref[...] = (dy * conv).astype(BF16)
    gk_ref[...] = (mid * v).astype(BF16)
    gv_ref[...] = (mid * k).astype(BF16)


def hyena_part(hyena_q, hyena_k, hyena_v, hyena_dy, filter_residue, filter_rate):
    length, chan_dev = hyena_q.shape
    modes, groups = filter_residue.shape
    size = chan_dev // groups
    spread = (groups, modes, size)
    rate_b = jnp.broadcast_to(filter_rate.T[:, :, None], spread)
    res_b = jnp.broadcast_to(filter_residue.T[:, :, None], spread)
    table = pl.BlockSpec((1, modes, size), lambda g: (g, 0, 0))
    rows = pl.BlockSpec((length, size), lambda g: (0, g))
    states = pl.pallas_call(
        state_kernel,
        grid=(groups,),
        in_specs=[table, rows, rows, rows, rows],
        out_specs=pl.BlockSpec((1, 2, modes, size), lambda g: (g, 0, 0, 0)),
        out_shape=jax.ShapeDtypeStruct((groups, 2, modes, size), F32),
        cost_estimate=pl.CostEstimate(
            flops=20 * modes * length * chan_dev,
            bytes_accessed=8 * length * chan_dev,
            transcendentals=0,
        ),
        name="hyena_state",
    )(rate_b, hyena_q, hyena_k, hyena_v, hyena_dy)
    everything = lax.all_gather(states, "ctx")
    count = everything.shape[0]
    me = lax.axis_index("ctx").astype(jnp.int32).reshape(1)
    out = jax.ShapeDtypeStruct((length, chan_dev), BF16)
    return pl.pallas_call(
        mix_kernel,
        grid=(groups,),
        in_specs=[
            pl.BlockSpec(memory_space=SMEM),
            table,
            table,
            pl.BlockSpec((count, 1, 2, modes, size), lambda g: (0, g, 0, 0, 0)),
            rows,
            rows,
            rows,
            rows,
        ],
        out_specs=[rows, rows, rows],
        out_shape=[out, out, out],
        cost_estimate=pl.CostEstimate(
            flops=24 * length * length * chan_dev,
            bytes_accessed=14 * length * chan_dev,
            transcendentals=0,
        ),
        name="hyena_mix",
    )(me, rate_b, res_b, everything, hyena_q, hyena_k, hyena_v, hyena_dy)


def attention_kernel(heads, share, tok_rows, *refs):
    places_ref, turn_ref = refs[:2]
    qkv_refs = refs[2 : 2 + share]
    grad_refs = refs[2 + share : 2 + 2 * share]
    out_refs = refs[2 + 2 * share : 2 + 3 * share]
    q_seq, k_seq, v_seq, g_seq, k_turn, delta_seq, score, dq_all, dk_all, dv_all = refs[
        2 + 3 * share :
    ]
    half_rows = tok_rows // 2
    scale = HD ** (-0.5)
    exp_scale = scale * math.log2(math.e)

    def rows_at(block, size):
        return pl.ds(pl.multiple_of(block * size, size), size)

    for part in range(share):

        def take(at, _, part=part):
            pieces = grad_refs[part][at, tok_rows:, :].astype(F32)
            for half in range(2):
                place = places_ref[0, (part * heads + at) * 2 + half]
                to = rows_at(place, half_rows)
                here = pl.ds(half * half_rows, half_rows)
                q_seq[to, :] = qkv_refs[part][at, 0, here, :]
                k_seq[to, :] = qkv_refs[part][at, 1, here, :]
                v_seq[to, :] = qkv_refs[part][at, 2, here, :]
                g_seq[to, :] = grad_refs[part][at, here, :]
                delta = pieces[half : half + 1] + pieces[2 + half : 3 + half]
                delta_seq[place, 0:1, :] = delta + pieces[4 + half : 5 + half]
            return 0

        lax.fori_loop(0, heads, take, 0)

    blocks = score.shape[0]

    def prepare(block, _):
        k_turn[block] = k_seq[rows_at(block, tok_rows), :].astype(F32).T.astype(BF16)
        zero = jnp.zeros((tok_rows, HD), F32)
        dq_all[rows_at(block, tok_rows), :] = zero
        dk_all[rows_at(block, tok_rows), :] = zero
        dv_all[rows_at(block, tok_rows), :] = zero
        return 0

    lax.fori_loop(0, blocks, prepare, 0)
    turn = turn_ref[0]
    square = (tok_rows, tok_rows)
    fold = (tok_rows // 8, 8, tok_rows)

    def one_block(step, _):
        even = step % 2 == 0
        mine = step * share + jnp.where(even, turn, share - 1 - turn)
        own = rows_at(mine, tok_rows)
        q = q_seq[own, :]
        g = g_seq[own, :]
        delta = jnp.concatenate(
            [delta_seq[2 * mine, 0:1, :], delta_seq[2 * mine + 1, 0:1, :]], axis=1
        )

        def fill(block, peak):
            s = dot_nt(k_seq[rows_at(block, tok_rows), :], q)
            score[block] = s
            return jnp.maximum(peak, jnp.max(s.reshape(fold), axis=0))

        peak = lax.fori_loop(0, mine, fill, jnp.full((8, tok_rows), NEG_LARGE, F32))
        s = dot_nt(k_seq[own, :], q)
        key_id = lax.broadcasted_iota(jnp.int32, square, 0)
        query_id = lax.broadcasted_iota(jnp.int32, square, 1)
        s = jnp.where(key_id <= query_id, s, NEG_LARGE)
        score[mine] = s
        peak = jnp.maximum(peak, jnp.max(s.reshape(fold), axis=0))
        peak = jnp.max(peak, axis=0, keepdims=True)

        def lift(block, total):
            e = jnp.exp2((score[block] - peak) * exp_scale)
            score[block] = e
            return total + jnp.sum(e.reshape(fold), axis=0)

        total = lax.fori_loop(0, mine + 1, lift, jnp.zeros((8, tok_rows), F32))
        inverse = 1.0 / jnp.sum(total, axis=0, keepdims=True)

        def spread(block, dq_turned):
            at = rows_at(block, tok_rows)
            probs = score[block] * inverse
            grad_prob = dot_nt(v_seq[at, :], g)
            grad_score = (probs * (grad_prob - delta)).astype(BF16)
            dv_all[at, :] += dot_nn(probs.astype(BF16), g)
            dk_all[at, :] += dot_nn(grad_score, q)
            return dq_turned + dot_nn(k_turn[block], grad_score)

        dq_turned = lax.fori_loop(0, mine + 1, spread, jnp.zeros((HD, tok_rows), F32))
        dq_all[own, :] = dq_turned.T
        return 0

    lax.fori_loop(0, heads, one_block, 0)

    for part in range(share):

        def give(at, _, part=part):
            for half in range(2):
                place = places_ref[1, (part * heads + at) * 2 + half]
                here = rows_at(place, half_rows)
                to = pl.ds(half * half_rows, half_rows)
                out_refs[part][at, 0, to, :] = dq_all[here, :] * scale
                out_refs[part][at, 1, to, :] = dk_all[here, :] * scale
                out_refs[part][at, 2, to, :] = dv_all[here, :]
            return 0

        lax.fori_loop(0, heads, give, 0)


def hop_heads(x, step, heads, share):
    pairs = [
        (h * share + j, ((h + step) % heads) * share + j)
        for h in range(heads)
        for j in range(share)
    ]
    return lax.ppermute(x, "ctx", pairs)


def hop_share(x, step, heads, share):
    pairs = [
        (h * share + j, h * share + (j + step) % share) for h in range(heads) for j in range(share)
    ]
    return lax.ppermute(x, "ctx", pairs)


def to_head(chunks, head, heads, share):
    got = []
    for step in range(heads):
        mine = lax.dynamic_index_in_dim(chunks, (head + step) % heads, 0, keepdims=False)
        got.append(mine if step == 0 else hop_heads(mine, step, heads, share))
    own = jnp.stack(got)
    return [own] + [hop_share(own, step, heads, share) for step in range(1, share)]


def attention_part(attn_q, attn_k, attn_v, grad_out, delta, block_place):
    tok_rows, feat_dev = attn_q.shape
    heads = feat_dev // HD
    count = lax.axis_size("ctx")
    share = count // heads
    index = lax.axis_index("ctx").astype(jnp.int32)
    head, turn = index // share, index % share

    def by_head(x):
        return x.reshape(x.shape[0], heads, HD).transpose(1, 0, 2)

    qkv = jnp.stack([by_head(attn_q), by_head(attn_k), by_head(attn_v)], axis=1)
    first = lax.reduce_precision(delta, 8, 7)
    left = delta - first
    second = lax.reduce_precision(left, 8, 7)
    third = left - second
    pieces = jnp.stack([first, second, third], axis=0).astype(BF16)
    pieces = pieces.transpose(2, 0, 1).reshape(heads, 3 * tok_rows // HD, HD)
    pad = jnp.zeros((heads, 16 - 3 * tok_rows // HD, HD), BF16)
    grads = jnp.concatenate([by_head(grad_out), pieces, pad], axis=1)
    qkv_parts = to_head(qkv, head, heads, share)
    grad_parts = to_head(grads, head, heads, share)

    part_id = jnp.arange(share, dtype=jnp.int32)[:, None]
    step_id = jnp.arange(heads, dtype=jnp.int32)[None, :]
    pairs = block_place.reshape(count, 2)
    sender = ((head - step_id) % heads) * share + (turn - part_id) % share
    receiver = ((head + step_id) % heads) * share + (turn + part_id) % share
    places = jnp.stack([pairs[sender].reshape(-1), pairs[receiver].reshape(-1)])

    total_rows = count * tok_rows
    vmem = pl.BlockSpec(memory_space=VMEM)
    smem = pl.BlockSpec(memory_space=SMEM)
    out = jax.ShapeDtypeStruct((heads, 3, tok_rows, HD), F32)
    low = pltpu.VMEM((total_rows, HD), BF16)
    full = pltpu.VMEM((total_rows, HD), F32)
    outs = pl.pallas_call(
        functools.partial(attention_kernel, heads, share, tok_rows),
        in_specs=[smem, smem] + [vmem] * (2 * share),
        out_specs=[vmem] * share,
        out_shape=[out] * share,
        scratch_shapes=[
            low,
            low,
            low,
            low,
            pltpu.VMEM((count, HD, tok_rows), BF16),
            pltpu.VMEM((2 * count, 8, HD), F32),
            pltpu.VMEM((count, tok_rows, tok_rows), F32),
            full,
            full,
            full,
        ],
        compiler_params=pltpu.CompilerParams(vmem_limit_bytes=60 * 1024 * 1024),
        cost_estimate=pl.CostEstimate(
            flops=10 * heads * tok_rows * total_rows * HD,
            bytes_accessed=20 * total_rows * HD,
            transcendentals=heads * tok_rows * total_rows // 2,
        ),
        name="attention_head",
    )(places, turn.reshape(1), *qkv_parts, *grad_parts)
    own = outs[0]
    for step in range(1, share):
        own = own + hop_share(outs[step], step, heads, share)
    own = own.astype(BF16)
    got = [own[0]] + [hop_heads(own[step], step, heads, share) for step in range(1, heads)]
    got = jnp.stack(got)
    got = got[(head - jnp.arange(heads, dtype=jnp.int32)) % heads]
    got = got.transpose(1, 2, 0, 3).reshape(3, tok_rows, feat_dev)
    return got[0], got[1], got[2]


def body(
    attn_q,
    attn_k,
    attn_v,
    attn_o,
    attn_dy,
    out_weight,
    block_place,
    hyena_q,
    hyena_k,
    hyena_v,
    hyena_dy,
    filter_residue,
    filter_rate,
):
    tok_rows, feat_dev = attn_q.shape
    heads_dev = feat_dev // HD
    grad_out = jnp.einsum(
        "tn,fn->tf",
        lax.all_gather(attn_dy, "tp", axis=1, tiled=True),
        out_weight,
        preferred_element_type=F32,
    ).astype(BF16)
    delta = jnp.sum(
        (grad_out.astype(F32) * attn_o.astype(F32)).reshape(tok_rows, heads_dev, HD), axis=2
    )
    grads_attn = attention_part(attn_q, attn_k, attn_v, grad_out, delta, block_place)
    grads_hyena = hyena_part(hyena_q, hyena_k, hyena_v, hyena_dy, filter_residue, filter_rate)
    return (*grads_attn, *grads_hyena)


def solution(mesh):
    both = P("ctx", "tp")
    in_specs = (both,) * 5 + (P("tp", None), P()) + (both,) * 4 + (P(None, "tp"),) * 2
    return jax.shard_map(
        body, mesh=mesh, in_specs=in_specs, out_specs=(both,) * 6, check_vma=False
    )
```

```python
import functools
import math

import jax
import jax.numpy as jnp
from jax import lax
from jax.experimental import pallas as pl
from jax.experimental.pallas import tpu as pltpu
from jax.sharding import PartitionSpec as P

HD = 128
NEG_LARGE = -1e30
F32 = jnp.float32
BF16 = jnp.bfloat16
VMEM = pltpu.MemorySpace.VMEM
SMEM = pltpu.MemorySpace.SMEM


def dot_nn(a, b, precision=None):
    return lax.dot_general(
        a, b, (((1,), (0,)), ((), ())), precision=precision, preferred_element_type=F32
    )


def dot_nt(a, b):
    return lax.dot_general(a, b, (((1,), (1,)), ((), ())), preferred_element_type=F32)


def wide(x, length):
    return jnp.concatenate([x] * (length // x.shape[1]), axis=1)


def state_kernel(rate_ref, q_ref, k_ref, v_ref, dy_ref, end_ref, begin_ref):
    length = q_ref.shape[0]
    highest = lax.Precision.HIGHEST
    rate = wide(rate_ref[0], length)
    lag = lax.broadcasted_iota(jnp.int32, rate.shape, 1).astype(F32)
    prod_kv = k_ref[...].astype(F32) * v_ref[...].astype(F32)
    prod_qdy = q_ref[...].astype(F32) * dy_ref[...].astype(F32)
    tail = jnp.exp(-rate * (length - 1 - lag))
    head = jnp.exp(-rate * lag)
    end_ref[0] = dot_nn(tail, prod_kv, highest)
    begin_ref[0] = dot_nn(head, prod_qdy, highest)


def mix_kernel(
    rate_ref, res_ref, in_ref, back_ref, q_ref, k_ref, v_ref, dy_ref, gq_ref, gk_ref, gv_ref
):
    length = q_ref.shape[0]
    highest = lax.Precision.HIGHEST
    rate = wide(rate_ref[0], length)
    res = wide(res_ref[0], length)
    lag_id = lax.broadcasted_iota(jnp.int32, rate.shape, 1)
    lag = lag_id.astype(F32)
    turned = jnp.where(lag_id == 0, 0, length - lag_id).astype(F32)
    taps = jnp.sum(res * jnp.exp(-rate * lag), axis=0, keepdims=True)
    taps_turned = jnp.sum(res * jnp.exp(-rate * turned), axis=0, keepdims=True)
    square = (length, length)
    row = lax.broadcasted_iota(jnp.int32, square, 0)
    col = lax.broadcasted_iota(jnp.int32, square, 1)
    lower = pltpu.roll(jnp.broadcast_to(taps_turned, square), 0, 1, stride=1, stride_axis=0)
    lower = jnp.where(col <= row, lower, 0.0)
    upper = pltpu.roll(jnp.broadcast_to(taps, square), 0, 1, stride=1, stride_axis=0)
    upper = jnp.where(col >= row, upper, 0.0)
    into = (res * jnp.exp(-rate * (lag + 1.0))).T
    back = (res * jnp.exp(-rate * (length - lag))).T
    k = k_ref[...].astype(F32)
    v = v_ref[...].astype(F32)
    dy = dy_ref[...].astype(F32)
    conv = dot_nn(lower, k * v, highest) + dot_nn(into, in_ref[0], highest)
    mid = dot_nn(upper, q_ref[...].astype(F32) * dy, highest) + dot_nn(back, back_ref[0], highest)
    gq_ref[...] = (dy * conv).astype(BF16)
    gk_ref[...] = (mid * v).astype(BF16)
    gv_ref[...] = (mid * k).astype(BF16)


def shifted(x, step):
    count = lax.axis_size("ctx")
    pairs = [(at, at + step) for at in range(count) if 0 <= at + step < count]
    return lax.ppermute(x, "ctx", pairs)


def earlier_and_later(states, filter_rate, length):
    count = lax.axis_size("ctx")
    ending, beginning = states
    state_in, state_back = shifted(ending, 1), shifted(beginning, -1)
    step = 1
    while step < count:
        decay = jnp.exp(-filter_rate.T * (step * length))[:, :, None]
        state_in = state_in + decay * shifted(state_in, step)
        state_back = state_back + decay * shifted(state_back, -step)
        step *= 2
    return state_in, state_back


def hyena_part(hyena_q, hyena_k, hyena_v, hyena_dy, filter_residue, filter_rate):
    length, chan_dev = hyena_q.shape
    modes, groups = filter_residue.shape
    size = chan_dev // groups
    spread = (groups, modes, size)
    rate_b = jnp.broadcast_to(filter_rate.T[:, :, None], spread)
    res_b = jnp.broadcast_to(filter_residue.T[:, :, None], spread)
    table = pl.BlockSpec((1, modes, size), lambda g: (g, 0, 0))
    rows = pl.BlockSpec((length, size), lambda g: (0, g))
    states = pl.pallas_call(
        state_kernel,
        grid=(groups,),
        in_specs=[table, rows, rows, rows, rows],
        out_specs=[table, table],
        out_shape=[jax.ShapeDtypeStruct(spread, F32)] * 2,
        cost_estimate=pl.CostEstimate(
            flops=20 * modes * length * chan_dev,
            bytes_accessed=8 * length * chan_dev,
            transcendentals=0,
        ),
        name="hyena_state",
    )(rate_b, hyena_q, hyena_k, hyena_v, hyena_dy)
    state_in, state_back = earlier_and_later(states, filter_rate, length)
    out = jax.ShapeDtypeStruct((length, chan_dev), BF16)
    return pl.pallas_call(
        mix_kernel,
        grid=(groups,),
        in_specs=[
            table,
            table,
            table,
            table,
            rows,
            rows,
            rows,
            rows,
        ],
        out_specs=[rows, rows, rows],
        out_shape=[out, out, out],
        cost_estimate=pl.CostEstimate(
            flops=24 * length * length * chan_dev,
            bytes_accessed=14 * length * chan_dev,
            transcendentals=0,
        ),
        name="hyena_mix",
    )(rate_b, res_b, state_in, state_back, hyena_q, hyena_k, hyena_v, hyena_dy)


def rows_at(block, size):
    return pl.ds(pl.multiple_of(block * size, size), size)


def own_block(step, share, turn):
    return step * share + jnp.where(step % 2 == 0, turn, share - 1 - turn)


def total_kernel(heads, share, tok_rows, places_ref, turn_ref, *refs):
    qkv_refs = refs[:share]
    log_ref, q_seq, k_seq, score = refs[share:]
    half_rows = tok_rows // 2
    exp_scale = HD ** (-0.5) * math.log2(math.e)
    for part in range(share):

        def take(at, _, part=part):
            for half in range(2):
                place = places_ref[0, (part * heads + at) * 2 + half]
                to = rows_at(place, half_rows)
                here = pl.ds(half * half_rows, half_rows)
                q_seq[to, :] = qkv_refs[part][at, 0, here, :]
                k_seq[to, :] = qkv_refs[part][at, 1, here, :]
            return 0

        lax.fori_loop(0, heads, take, 0)
    turn = turn_ref[0]
    square = (tok_rows, tok_rows)
    fold = (tok_rows // 8, 8, tok_rows)

    def one_block(step, _):
        mine = own_block(step, share, turn)
        own = rows_at(mine, tok_rows)
        q = q_seq[own, :]

        def fill(block, peak):
            s = dot_nt(k_seq[rows_at(block, tok_rows), :], q)
            score[block] = s
            return jnp.maximum(peak, jnp.max(s.reshape(fold), axis=0))

        peak = lax.fori_loop(0, mine, fill, jnp.full((8, tok_rows), NEG_LARGE, F32))
        s = dot_nt(k_seq[own, :], q)
        key_id = lax.broadcasted_iota(jnp.int32, square, 0)
        query_id = lax.broadcasted_iota(jnp.int32, square, 1)
        s = jnp.where(key_id <= query_id, s, NEG_LARGE)
        score[mine] = s
        peak = jnp.maximum(peak, jnp.max(s.reshape(fold), axis=0))
        peak = jnp.max(peak, axis=0, keepdims=True)

        def lift(block, total):
            e = jnp.exp2((score[block] - peak) * exp_scale)
            return total + jnp.sum(e.reshape(fold), axis=0)

        total = lax.fori_loop(0, mine + 1, lift, jnp.zeros((8, tok_rows), F32))
        total = jnp.sum(total, axis=0, keepdims=True)
        log_total = peak * exp_scale + jnp.log2(total)
        log_ref[step] = jnp.broadcast_to(log_total, (8, tok_rows))
        return 0

    lax.fori_loop(0, heads, one_block, 0)


def attention_kernel(heads, share, tok_rows, *refs):
    places_ref, turn_ref, log_ref = refs[:3]
    qkv_refs = refs[3 : 3 + share]
    grad_refs = refs[3 + share : 3 + 2 * share]
    out_refs = refs[3 + 2 * share : 3 + 3 * share]
    q_seq, k_seq, v_seq, g_seq, k_turn, delta_seq, dq_all, dk_all, dv_all = refs[3 + 3 * share :]
    half_rows = tok_rows // 2
    scale = HD ** (-0.5)
    exp_scale = scale * math.log2(math.e)
    for part in range(share):

        def take(at, _, part=part):
            pieces = grad_refs[part][at, tok_rows:, :].astype(F32)
            for half in range(2):
                place = places_ref[0, (part * heads + at) * 2 + half]
                to = rows_at(place, half_rows)
                here = pl.ds(half * half_rows, half_rows)
                q_seq[to, :] = qkv_refs[part][at, 0, here, :]
                k_seq[to, :] = qkv_refs[part][at, 1, here, :]
                v_seq[to, :] = qkv_refs[part][at, 2, here, :]
                g_seq[to, :] = grad_refs[part][at, here, :]
                delta = pieces[half : half + 1] + pieces[2 + half : 3 + half]
                delta_seq[place, 0:1, :] = delta + pieces[4 + half : 5 + half]
            return 0

        lax.fori_loop(0, heads, take, 0)

    def prepare(block, _):
        k_turn[block] = k_seq[rows_at(block, tok_rows), :].astype(F32).T.astype(BF16)
        zero = jnp.zeros((tok_rows, HD), F32)
        dq_all[rows_at(block, tok_rows), :] = zero
        dk_all[rows_at(block, tok_rows), :] = zero
        dv_all[rows_at(block, tok_rows), :] = zero
        return 0

    lax.fori_loop(0, k_turn.shape[0], prepare, 0)
    turn = turn_ref[0]
    square = (tok_rows, tok_rows)

    def one_block(step, _):
        mine = own_block(step, share, turn)
        own = rows_at(mine, tok_rows)
        q = q_seq[own, :]
        g = g_seq[own, :]
        log_total = log_ref[step, 0:1, :]
        delta = jnp.concatenate(
            [delta_seq[2 * mine, 0:1, :], delta_seq[2 * mine + 1, 0:1, :]], axis=1
        )

        def spread(block, dq_turned, masked=False):
            at = rows_at(block, tok_rows)
            exponent = dot_nt(k_seq[at, :], q) * exp_scale - log_total
            if masked:
                key_id = lax.broadcasted_iota(jnp.int32, square, 0)
                query_id = lax.broadcasted_iota(jnp.int32, square, 1)
                exponent = jnp.where(key_id <= query_id, exponent, NEG_LARGE)
            probs = jnp.exp2(exponent)
            grad_prob = dot_nt(v_seq[at, :], g)
            grad_score = (probs * (grad_prob - delta)).astype(BF16)
            dv_all[at, :] += dot_nn(probs.astype(BF16), g)
            dk_all[at, :] += dot_nn(grad_score, q)
            return dq_turned + dot_nn(k_turn[block], grad_score)

        def two(pair, dq_turned):
            return spread(2 * pair + 1, spread(2 * pair, dq_turned))

        dq_turned = lax.fori_loop(0, mine // 2, two, jnp.zeros((HD, tok_rows), F32))
        dq_turned = lax.fori_loop(mine // 2 * 2, mine, spread, dq_turned)
        dq_turned = spread(mine, dq_turned, True)
        dq_all[own, :] = dq_turned.T
        return 0

    lax.fori_loop(0, heads, one_block, 0)

    for part in range(share):

        def give(at, _, part=part):
            for half in range(2):
                place = places_ref[1, (part * heads + at) * 2 + half]
                here = rows_at(place, half_rows)
                to = pl.ds(half * half_rows, half_rows)
                out_refs[part][at, 0, to, :] = dq_all[here, :] * scale
                out_refs[part][at, 1, to, :] = dk_all[here, :] * scale
                out_refs[part][at, 2, to, :] = dv_all[here, :]
            return 0

        lax.fori_loop(0, heads, give, 0)


def hop_heads(x, step, heads, share):
    pairs = [
        (h * share + j, ((h + step) % heads) * share + j)
        for h in range(heads)
        for j in range(share)
    ]
    return lax.ppermute(x, "ctx", pairs)


def hop_share(x, step, heads, share):
    pairs = [
        (h * share + j, h * share + (j + step) % share) for h in range(heads) for j in range(share)
    ]
    return lax.ppermute(x, "ctx", pairs)


def to_head(chunks, head, heads, share):
    got = []
    for step in range(heads):
        mine = lax.dynamic_index_in_dim(chunks, (head + step) % heads, 0, keepdims=False)
        got.append(mine if step == 0 else hop_heads(mine, step, heads, share))
    own = jnp.stack(got)
    return [own] + [hop_share(own, step, heads, share) for step in range(1, share)]


def attention_part(attn_q, attn_k, attn_v, grad_out, delta, block_place):
    tok_rows, feat_dev = attn_q.shape
    heads = feat_dev // HD
    count = lax.axis_size("ctx")
    share = count // heads
    index = lax.axis_index("ctx").astype(jnp.int32)
    head, turn = index // share, index % share

    def by_head(x):
        return x.reshape(x.shape[0], heads, HD).transpose(1, 0, 2)

    qkv = jnp.stack([by_head(attn_q), by_head(attn_k), by_head(attn_v)], axis=1)
    first = lax.reduce_precision(delta, 8, 7)
    left = delta - first
    second = lax.reduce_precision(left, 8, 7)
    third = left - second
    pieces = jnp.stack([first, second, third], axis=0).astype(BF16)
    pieces = pieces.transpose(2, 0, 1).reshape(heads, 3 * tok_rows // HD, HD)
    pad = jnp.zeros((heads, 16 - 3 * tok_rows // HD, HD), BF16)
    grads = jnp.concatenate([by_head(grad_out), pieces, pad], axis=1)
    qkv_parts = to_head(qkv, head, heads, share)
    grad_parts = to_head(grads, head, heads, share)

    part_id = jnp.arange(share, dtype=jnp.int32)[:, None]
    step_id = jnp.arange(heads, dtype=jnp.int32)[None, :]
    pairs = block_place.reshape(count, 2)
    sender = ((head - step_id) % heads) * share + (turn - part_id) % share
    receiver = ((head + step_id) % heads) * share + (turn + part_id) % share
    places = jnp.stack([pairs[sender].reshape(-1), pairs[receiver].reshape(-1)])

    total_rows = count * tok_rows
    vmem = pl.BlockSpec(memory_space=VMEM)
    smem = pl.BlockSpec(memory_space=SMEM)
    out = jax.ShapeDtypeStruct((heads, 3, tok_rows, HD), F32)
    low = pltpu.VMEM((total_rows, HD), BF16)
    full = pltpu.VMEM((total_rows, HD), F32)
    log_total = pl.pallas_call(
        functools.partial(total_kernel, heads, share, tok_rows),
        in_specs=[smem, smem] + [vmem] * share,
        out_specs=vmem,
        out_shape=jax.ShapeDtypeStruct((heads, 8, tok_rows), F32),
        scratch_shapes=[low, low, pltpu.VMEM((count, tok_rows, tok_rows), F32)],
        compiler_params=pltpu.CompilerParams(vmem_limit_bytes=40 * 1024 * 1024),
        cost_estimate=pl.CostEstimate(
            flops=2 * heads * tok_rows * total_rows * HD,
            bytes_accessed=6 * total_rows * HD,
            transcendentals=heads * tok_rows * total_rows // 2,
        ),
        name="log_total",
    )(places, turn.reshape(1), *qkv_parts)
    outs = pl.pallas_call(
        functools.partial(attention_kernel, heads, share, tok_rows),
        in_specs=[smem, smem, vmem] + [vmem] * (2 * share),
        out_specs=[vmem] * share,
        out_shape=[out] * share,
        scratch_shapes=[
            low,
            low,
            low,
            low,
            pltpu.VMEM((count, HD, tok_rows), BF16),
            pltpu.VMEM((2 * count, 8, HD), F32),
            full,
            full,
            full,
        ],
        compiler_params=pltpu.CompilerParams(vmem_limit_bytes=60 * 1024 * 1024),
        cost_estimate=pl.CostEstimate(
            flops=10 * heads * tok_rows * total_rows * HD,
            bytes_accessed=20 * total_rows * HD,
            transcendentals=heads * tok_rows * total_rows // 2,
        ),
        name="attention_head",
    )(places, turn.reshape(1), log_total, *qkv_parts, *grad_parts)
    own = outs[0]
    for step in range(1, share):
        own = own + hop_share(outs[step], step, heads, share)
    own = own.astype(BF16)
    got = [own[0]] + [hop_heads(own[step], step, heads, share) for step in range(1, heads)]
    got = jnp.stack(got)
    got = got[(head - jnp.arange(heads, dtype=jnp.int32)) % heads]
    got = got.transpose(1, 2, 0, 3).reshape(3, tok_rows, feat_dev)
    return got[0], got[1], got[2]


def body(
    attn_q,
    attn_k,
    attn_v,
    attn_o,
    attn_dy,
    out_weight,
    block_place,
    hyena_q,
    hyena_k,
    hyena_v,
    hyena_dy,
    filter_residue,
    filter_rate,
):
    tok_rows, feat_dev = attn_q.shape
    heads_dev = feat_dev // HD
    parts = lax.axis_size("tp")
    at = lax.axis_index("tp")
    width = attn_dy.shape[1]
    pieces = [attn_dy]
    for step in range(1, parts):
        pairs = [((j + step) % parts, j) for j in range(parts)]
        pieces.append(lax.ppermute(attn_dy, "tp", pairs))
    grad_out = None
    for step, piece in enumerate(pieces):
        weight = lax.dynamic_slice_in_dim(out_weight, (at + step) % parts * width, width, 1)
        term = jnp.einsum("tn,fn->tf", piece, weight, preferred_element_type=F32)
        grad_out = term if grad_out is None else grad_out + term
    grad_out = grad_out.astype(BF16)
    delta = jnp.sum(
        (grad_out.astype(F32) * attn_o.astype(F32)).reshape(tok_rows, heads_dev, HD), axis=2
    )
    grads_attn = attention_part(attn_q, attn_k, attn_v, grad_out, delta, block_place)
    grads_hyena = hyena_part(hyena_q, hyena_k, hyena_v, hyena_dy, filter_residue, filter_rate)
    return (*grads_attn, *grads_hyena)


def solution(mesh):
    both = P("ctx", "tp")
    in_specs = (both,) * 5 + (P("tp", None), P()) + (both,) * 4 + (P(None, "tp"),) * 2
    return jax.shard_map(
        body, mesh=mesh, in_specs=in_specs, out_specs=(both,) * 6, check_vma=False
    )
```

```python
import functools
import math

import jax
import jax.numpy as jnp
from jax import lax
from jax.experimental import pallas as pl
from jax.experimental.pallas import tpu as pltpu
from jax.sharding import PartitionSpec as P


HD = 128
NEG_LARGE = -1e30
F32 = jnp.float32
BF16 = jnp.bfloat16
VMEM = pltpu.MemorySpace.VMEM
SMEM = pltpu.MemorySpace.SMEM


def dot_nn(a, b, precision=None):
    return lax.dot_general(
        a, b, (((1,), (0,)), ((), ())), precision=precision, preferred_element_type=F32
    )


def dot_nt(a, b):
    return lax.dot_general(a, b, (((1,), (1,)), ((), ())), preferred_element_type=F32)


def wide(x, length):
    return jnp.concatenate([x] * (length // x.shape[1]), axis=1)


def state_kernel(rate_ref, q_ref, k_ref, v_ref, dy_ref, out_ref):
    length = q_ref.shape[0]
    highest = lax.Precision.HIGHEST
    rate = wide(rate_ref[0], length)
    lag = lax.broadcasted_iota(jnp.int32, rate.shape, 1).astype(F32)
    prod_kv = k_ref[...].astype(F32) * v_ref[...].astype(F32)
    prod_qdy = q_ref[...].astype(F32) * dy_ref[...].astype(F32)
    tail = jnp.exp(-rate * (length - 1 - lag))
    head = jnp.exp(-rate * lag)
    out_ref[0, 0] = dot_nn(tail, prod_kv, highest)
    out_ref[0, 1] = dot_nn(head, prod_qdy, highest)


def mix_kernel(
    me_ref, rate_ref, res_ref, all_ref, q_ref, k_ref, v_ref, dy_ref, gq_ref, gk_ref, gv_ref
):
    length = q_ref.shape[0]
    count = all_ref.shape[0]
    highest = lax.Precision.HIGHEST
    me = me_ref[0]
    rate_b = rate_ref[0]
    state_in = jnp.zeros(rate_b.shape, F32)
    state_back = jnp.zeros(rate_b.shape, F32)
    for at in range(count):
        gap = me - 1 - at
        weight = jnp.exp(-rate_b * (length * jnp.maximum(gap, 0)).astype(F32))
        state_in = state_in + jnp.where(gap >= 0, weight, 0.0) * all_ref[at, 0, 0]
        gap = at - 1 - me
        weight = jnp.exp(-rate_b * (length * jnp.maximum(gap, 0)).astype(F32))
        state_back = state_back + jnp.where(gap >= 0, weight, 0.0) * all_ref[at, 0, 1]
    rate = wide(rate_b, length)
    res = wide(res_ref[0], length)
    lag_id = lax.broadcasted_iota(jnp.int32, rate.shape, 1)
    lag = lag_id.astype(F32)
    turned = jnp.where(lag_id == 0, 0, length - lag_id).astype(F32)
    taps = jnp.sum(res * jnp.exp(-rate * lag), axis=0, keepdims=True)
    taps_turned = jnp.sum(res * jnp.exp(-rate * turned), axis=0, keepdims=True)
    square = (length, length)
    row = lax.broadcasted_iota(jnp.int32, square, 0)
    col = lax.broadcasted_iota(jnp.int32, square, 1)
    lower = pltpu.roll(jnp.broadcast_to(taps_turned, square), 0, 1, stride=1, stride_axis=0)
    lower = jnp.where(col <= row, lower, 0.0)
    upper = pltpu.roll(jnp.broadcast_to(taps, square), 0, 1, stride=1, stride_axis=0)
    upper = jnp.where(col >= row, upper, 0.0)
    into = (res * jnp.exp(-rate * (lag + 1.0))).T
    back = (res * jnp.exp(-rate * (length - lag))).T
    k = k_ref[...].astype(F32)
    v = v_ref[...].astype(F32)
    dy = dy_ref[...].astype(F32)
    conv = dot_nn(lower, k * v, highest) + dot_nn(into, state_in, highest)
    mid = dot_nn(upper, q_ref[...].astype(F32) * dy, highest) + dot_nn(back, state_back, highest)
    gq_ref[...] = (dy * conv).astype(BF16)
    gk_ref[...] = (mid * v).astype(BF16)
    gv_ref[...] = (mid * k).astype(BF16)


def hyena_part(hyena_q, hyena_k, hyena_v, hyena_dy, filter_residue, filter_rate):
    length, chan_dev = hyena_q.shape
    modes, groups = filter_residue.shape
    size = chan_dev // groups
    spread = (groups, modes, size)
    rate_b = jnp.broadcast_to(filter_rate.T[:, :, None], spread)
    res_b = jnp.broadcast_to(filter_residue.T[:, :, None], spread)
    table = pl.BlockSpec((1, modes, size), lambda g: (g, 0, 0))
    rows = pl.BlockSpec((length, size), lambda g: (0, g))
    states = pl.pallas_call(
        state_kernel,
        grid=(groups,),
        in_specs=[table, rows, rows, rows, rows],
        out_specs=pl.BlockSpec((1, 2, modes, size), lambda g: (g, 0, 0, 0)),
        out_shape=jax.ShapeDtypeStruct((groups, 2, modes, size), F32),
        cost_estimate=pl.CostEstimate(
            flops=20 * modes * length * chan_dev,
            bytes_accessed=8 * length * chan_dev,
            transcendentals=0,
        ),
        name="hyena_state",
    )(rate_b, hyena_q, hyena_k, hyena_v, hyena_dy)
    everything = lax.all_gather(states, "ctx")
    count = everything.shape[0]
    me = lax.axis_index("ctx").astype(jnp.int32).reshape(1)
    out = jax.ShapeDtypeStruct((length, chan_dev), BF16)
    return pl.pallas_call(
        mix_kernel,
        grid=(groups,),
        in_specs=[
            pl.BlockSpec(memory_space=SMEM),
            table,
            table,
            pl.BlockSpec((count, 1, 2, modes, size), lambda g: (0, g, 0, 0, 0)),
            rows,
            rows,
            rows,
            rows,
        ],
        out_specs=[rows, rows, rows],
        out_shape=[out, out, out],
        cost_estimate=pl.CostEstimate(
            flops=24 * length * length * chan_dev,
            bytes_accessed=14 * length * chan_dev,
            transcendentals=0,
        ),
        name="hyena_mix",
    )(me, rate_b, res_b, everything, hyena_q, hyena_k, hyena_v, hyena_dy)


def rows_at(block, size):
    return pl.ds(pl.multiple_of(block * size, size), size)


def own_block(step, share, turn):
    return step * share + jnp.where(step % 2 == 0, turn, share - 1 - turn)


def total_kernel(heads, share, tok_rows, places_ref, turn_ref, *refs):
    qkv_refs = refs[:share]
    log_ref, q_seq, k_seq, score = refs[share:]
    half_rows = tok_rows // 2
    exp_scale = HD ** (-0.5) * math.log2(math.e)
    for part in range(share):

        def take(at, _, part=part):
            for half in range(2):
                place = places_ref[0, (part * heads + at) * 2 + half]
                to = rows_at(place, half_rows)
                here = pl.ds(half * half_rows, half_rows)
                q_seq[to, :] = qkv_refs[part][at, 0, here, :]
                k_seq[to, :] = qkv_refs[part][at, 1, here, :]
            return 0

        lax.fori_loop(0, heads, take, 0)
    turn = turn_ref[0]
    square = (tok_rows, tok_rows)
    fold = (tok_rows // 8, 8, tok_rows)

    def one_block(step, _):
        mine = own_block(step, share, turn)
        own = rows_at(mine, tok_rows)
        q = q_seq[own, :]

        def fill(block, peak):
            s = dot_nt(k_seq[rows_at(block, tok_rows), :], q)
            score[block] = s
            return jnp.maximum(peak, jnp.max(s.reshape(fold), axis=0))

        peak = lax.fori_loop(0, mine, fill, jnp.full((8, tok_rows), NEG_LARGE, F32))
        s = dot_nt(k_seq[own, :], q)
        key_id = lax.broadcasted_iota(jnp.int32, square, 0)
        query_id = lax.broadcasted_iota(jnp.int32, square, 1)
        s = jnp.where(key_id <= query_id, s, NEG_LARGE)
        score[mine] = s
        peak = jnp.maximum(peak, jnp.max(s.reshape(fold), axis=0))
        peak = jnp.max(peak, axis=0, keepdims=True)

        def lift(block, total):
            e = jnp.exp2((score[block] - peak) * exp_scale)
            return total + jnp.sum(e.reshape(fold), axis=0)

        total = lax.fori_loop(0, mine + 1, lift, jnp.zeros((8, tok_rows), F32))
        total = jnp.sum(total, axis=0, keepdims=True)
        log_total = peak * exp_scale + jnp.log2(total)
        log_ref[step] = jnp.broadcast_to(log_total, (8, tok_rows))
        return 0

    lax.fori_loop(0, heads, one_block, 0)


def attention_kernel(heads, share, tok_rows, *refs):
    places_ref, turn_ref, log_ref = refs[:3]
    qkv_refs = refs[3 : 3 + share]
    grad_refs = refs[3 + share : 3 + 2 * share]
    out_refs = refs[3 + 2 * share : 3 + 3 * share]
    q_seq, k_seq, v_seq, g_seq, k_turn, delta_seq, dq_all, dk_all, dv_all = refs[3 + 3 * share :]
    half_rows = tok_rows // 2
    scale = HD ** (-0.5)
    exp_scale = scale * math.log2(math.e)
    for part in range(share):

        def take(at, _, part=part):
            pieces = grad_refs[part][at, tok_rows:, :].astype(F32)
            for half in range(2):
                place = places_ref[0, (part * heads + at) * 2 + half]
                to = rows_at(place, half_rows)
                here = pl.ds(half * half_rows, half_rows)
                q_seq[to, :] = qkv_refs[part][at, 0, here, :]
                k_seq[to, :] = qkv_refs[part][at, 1, here, :]
                v_seq[to, :] = qkv_refs[part][at, 2, here, :]
                g_seq[to, :] = grad_refs[part][at, here, :]
                delta = pieces[half : half + 1] + pieces[2 + half : 3 + half]
                delta_seq[place, 0:1, :] = delta + pieces[4 + half : 5 + half]
            return 0

        lax.fori_loop(0, heads, take, 0)

    def prepare(block, _):
        k_turn[block] = k_seq[rows_at(block, tok_rows), :].astype(F32).T.astype(BF16)
        zero = jnp.zeros((tok_rows, HD), F32)
        dq_all[rows_at(block, tok_rows), :] = zero
        dk_all[rows_at(block, tok_rows), :] = zero
        dv_all[rows_at(block, tok_rows), :] = zero
        return 0

    lax.fori_loop(0, k_turn.shape[0], prepare, 0)
    turn = turn_ref[0]
    square = (tok_rows, tok_rows)

    def one_block(step, _):
        mine = own_block(step, share, turn)
        own = rows_at(mine, tok_rows)
        q = q_seq[own, :]
        g = g_seq[own, :]
        log_total = log_ref[step, 0:1, :]
        delta = jnp.concatenate(
            [delta_seq[2 * mine, 0:1, :], delta_seq[2 * mine + 1, 0:1, :]], axis=1
        )

        def spread(block, dq_turned, masked=False):
            at = rows_at(block, tok_rows)
            exponent = dot_nt(k_seq[at, :], q) * exp_scale - log_total
            if masked:
                key_id = lax.broadcasted_iota(jnp.int32, square, 0)
                query_id = lax.broadcasted_iota(jnp.int32, square, 1)
                exponent = jnp.where(key_id <= query_id, exponent, NEG_LARGE)
            probs = jnp.exp2(exponent)
            grad_prob = dot_nt(v_seq[at, :], g)
            grad_score = (probs * (grad_prob - delta)).astype(BF16)
            dv_all[at, :] += dot_nn(probs.astype(BF16), g)
            dk_all[at, :] += dot_nn(grad_score, q)
            return dq_turned + dot_nn(k_turn[block], grad_score)

        def two(pair, dq_turned):
            return spread(2 * pair + 1, spread(2 * pair, dq_turned))

        dq_turned = lax.fori_loop(0, mine // 2, two, jnp.zeros((HD, tok_rows), F32))
        dq_turned = lax.fori_loop(mine // 2 * 2, mine, spread, dq_turned)
        dq_turned = spread(mine, dq_turned, True)
        dq_all[own, :] = dq_turned.T
        return 0

    lax.fori_loop(0, heads, one_block, 0)

    for part in range(share):

        def give(at, _, part=part):
            for half in range(2):
                place = places_ref[1, (part * heads + at) * 2 + half]
                here = rows_at(place, half_rows)
                to = pl.ds(half * half_rows, half_rows)
                out_refs[part][at, 0, to, :] = dq_all[here, :] * scale
                out_refs[part][at, 1, to, :] = dk_all[here, :] * scale
                out_refs[part][at, 2, to, :] = dv_all[here, :]
            return 0

        lax.fori_loop(0, heads, give, 0)


def hop_heads(x, step, heads, share):
    pairs = [
        (h * share + j, ((h + step) % heads) * share + j)
        for h in range(heads)
        for j in range(share)
    ]
    return lax.ppermute(x, "ctx", pairs)


def hop_share(x, step, heads, share):
    pairs = [
        (h * share + j, h * share + (j + step) % share) for h in range(heads) for j in range(share)
    ]
    return lax.ppermute(x, "ctx", pairs)


def to_head(chunks, head, heads, share):
    got = []
    for step in range(heads):
        mine = lax.dynamic_index_in_dim(chunks, (head + step) % heads, 0, keepdims=False)
        got.append(mine if step == 0 else hop_heads(mine, step, heads, share))
    own = jnp.stack(got)
    return [own] + [hop_share(own, step, heads, share) for step in range(1, share)]


def attention_part(attn_q, attn_k, attn_v, grad_out, delta, block_place):
    tok_rows, feat_dev = attn_q.shape
    heads = feat_dev // HD
    count = lax.axis_size("ctx")
    share = count // heads
    index = lax.axis_index("ctx").astype(jnp.int32)
    head, turn = index // share, index % share

    def by_head(x):
        return x.reshape(x.shape[0], heads, HD).transpose(1, 0, 2)

    qkv = jnp.stack([by_head(attn_q), by_head(attn_k), by_head(attn_v)], axis=1)
    first = lax.reduce_precision(delta, 8, 7)
    left = delta - first
    second = lax.reduce_precision(left, 8, 7)
    third = left - second
    pieces = jnp.stack([first, second, third], axis=0).astype(BF16)
    pieces = pieces.transpose(2, 0, 1).reshape(heads, 3 * tok_rows // HD, HD)
    pad = jnp.zeros((heads, 16 - 3 * tok_rows // HD, HD), BF16)
    grads = jnp.concatenate([by_head(grad_out), pieces, pad], axis=1)
    qkv_parts = to_head(qkv, head, heads, share)
    grad_parts = to_head(grads, head, heads, share)

    part_id = jnp.arange(share, dtype=jnp.int32)[:, None]
    step_id = jnp.arange(heads, dtype=jnp.int32)[None, :]
    pairs = block_place.reshape(count, 2)
    sender = ((head - step_id) % heads) * share + (turn - part_id) % share
    receiver = ((head + step_id) % heads) * share + (turn + part_id) % share
    places = jnp.stack([pairs[sender].reshape(-1), pairs[receiver].reshape(-1)])

    total_rows = count * tok_rows
    vmem = pl.BlockSpec(memory_space=VMEM)
    smem = pl.BlockSpec(memory_space=SMEM)
    out = jax.ShapeDtypeStruct((heads, 3, tok_rows, HD), F32)
    low = pltpu.VMEM((total_rows, HD), BF16)
    full = pltpu.VMEM((total_rows, HD), F32)
    log_total = pl.pallas_call(
        functools.partial(total_kernel, heads, share, tok_rows),
        in_specs=[smem, smem] + [vmem] * share,
        out_specs=vmem,
        out_shape=jax.ShapeDtypeStruct((heads, 8, tok_rows), F32),
        scratch_shapes=[low, low, pltpu.VMEM((count, tok_rows, tok_rows), F32)],
        compiler_params=pltpu.CompilerParams(vmem_limit_bytes=40 * 1024 * 1024),
        cost_estimate=pl.CostEstimate(
            flops=2 * heads * tok_rows * total_rows * HD,
            bytes_accessed=6 * total_rows * HD,
            transcendentals=heads * tok_rows * total_rows // 2,
        ),
        name="log_total",
    )(places, turn.reshape(1), *qkv_parts)
    outs = pl.pallas_call(
        functools.partial(attention_kernel, heads, share, tok_rows),
        in_specs=[smem, smem, vmem] + [vmem] * (2 * share),
        out_specs=[vmem] * share,
        out_shape=[out] * share,
        scratch_shapes=[
            low,
            low,
            low,
            low,
            pltpu.VMEM((count, HD, tok_rows), BF16),
            pltpu.VMEM((2 * count, 8, HD), F32),
            full,
            full,
            full,
        ],
        compiler_params=pltpu.CompilerParams(vmem_limit_bytes=60 * 1024 * 1024),
        cost_estimate=pl.CostEstimate(
            flops=10 * heads * tok_rows * total_rows * HD,
            bytes_accessed=20 * total_rows * HD,
            transcendentals=heads * tok_rows * total_rows // 2,
        ),
        name="attention_head",
    )(places, turn.reshape(1), log_total, *qkv_parts, *grad_parts)
    own = outs[0]
    for step in range(1, share):
        own = own + hop_share(outs[step], step, heads, share)
    own = own.astype(BF16)
    got = [own[0]]
    for step in range(1, heads):
        got.append(hop_heads(own[step], step, heads, share))
    got = jnp.stack(got)
    got = got[(head - jnp.arange(heads, dtype=jnp.int32)) % heads]
    got = got.transpose(1, 2, 0, 3).reshape(3, tok_rows, feat_dev)
    return got[0], got[1], got[2]


def all_grads(
    attn_q,
    attn_k,
    attn_v,
    attn_o,
    attn_dy,
    out_weight,
    block_place,
    hyena_q,
    hyena_k,
    hyena_v,
    hyena_dy,
    filter_residue,
    filter_rate,
):
    tok_rows, feat_dev = attn_q.shape
    heads_dev = feat_dev // HD
    parts = lax.axis_size("tp")
    at = lax.axis_index("tp")
    width = attn_dy.shape[1]
    pieces = [attn_dy]
    for step in range(1, parts):
        pairs = [((j + step) % parts, j) for j in range(parts)]
        pieces.append(lax.ppermute(attn_dy, "tp", pairs))
    grad_out = None
    for step, piece in enumerate(pieces):
        weight = lax.dynamic_slice_in_dim(out_weight, (at + step) % parts * width, width, 1)
        term = jnp.einsum("tn,fn->tf", piece, weight, preferred_element_type=F32)
        grad_out = term if grad_out is None else grad_out + term
    grad_out = grad_out.astype(BF16)
    delta = jnp.sum(
        (grad_out.astype(F32) * attn_o.astype(F32)).reshape(tok_rows, heads_dev, HD), axis=2
    )
    grads_attn = attention_part(attn_q, attn_k, attn_v, grad_out, delta, block_place)
    grads_hyena = hyena_part(hyena_q, hyena_k, hyena_v, hyena_dy, filter_residue, filter_rate)
    return (*grads_attn, *grads_hyena)


def solution(mesh):
    both = P("ctx", "tp")
    in_specs = (both,) * 5 + (P("tp", None), P()) + (both,) * 4 + (P(None, "tp"),) * 2
    return jax.shard_map(
        all_grads, mesh=mesh, in_specs=in_specs, out_specs=(both,) * 6, check_vma=False
    )
```
